128 devices in a mesh: row: 8 (over y, z_hi), col: 16 (over x, z_lo, core).
Axes of the slice: x: 4, y: 4, z: 4 (z_hi: 2, z_lo: 2; z = z_hi * 2 + z_lo), core: 2. Of those that a mesh axis runs over, the one named last changes fastest.
Arguments:
- factor_blocks: bfloat16 [6, 4, 2048, 2, 4096], P(None, None, 'row', None, 'col'), may hold values from -0.03125 to 0.03125
- inverse_blocks: bfloat16 [4, 2, 4096, 4, 2048], P(None, None, 'col', None, 'row'), as said below
- right_side: bfloat16 [4, 4, 2048, 128], P(None, None, 'row'), may hold values from -4 to 4
- centers: bfloat16 [8, 4096, 512], P(None, 'col')
- owner_map: int32 [8, 16], P(None, 'col'), may hold values from 0 to 7, as said below
- test_pool: bfloat16 [49152, 512], P('row')
- test_rows: int32 [32768], P('row'), may hold values from 0 to 49151, as said below
Outputs:
- coefficients: float32 [4, 2, 4096, 128], P(None, None, 'col')
- predictions: float32 [32768, 128], P(('row', 'col'))
The draws below stay inside these ranges and needn't reach their ends.
Inputs may be any that keep to these rules, and one draw needn't show every extreme that they name: `owner_map`: each column c is a permutation of 0 to 7. `test_rows`: entry i names a row of block i // 4096 of the pool, that is from (i // 4096) * 6144 to (i // 4096 + 1) * 6144 - 1; rows may repeat. `inverse_blocks`: read as D_k, each block is upper triangular with a positive diagonal.
All inputs are finite; a program needn't handle non-finite values.
Results may differ from the reference program's by a relative error of at most 0.019.
Values may be sent and summed in bfloat16 or wider, within the bound.
A program may use at most 128 MiB of HBM per device.

```python
import jax
import jax.numpy as jnp
from jax import lax

PANEL = 8192
TILE = 256
NP = 4
DIM = 512
OUT = 128
TEST_DEV = 4096
TPP = 32
RT = 4
CT = 2
NLOC = 8
PAIRS = 6
POOL_DEV = 6144
POOL = 49152
NTEST = 32768
N_ROW = 8
N_COL = 16


def point_cloud(key, amount):
    feature = jnp.arange(DIM, dtype=jnp.float32)
    spread = 1.0 / jnp.sqrt(feature + 1.0)
    values = jax.random.normal(key, (amount, DIM), jnp.float32) * spread[None, :]
    return values


def draw_centers(key, part):
    values = point_cloud(jax.random.fold_in(key, 11), NP * PANEL)
    return values.reshape(NLOC, NP * PANEL // NLOC, DIM).astype(jnp.bfloat16)


def draw_test_pool(key, part):
    return point_cloud(jax.random.fold_in(key, 13), POOL).astype(jnp.bfloat16)


def draw_inverse_blocks(key, part):
    col_count = TPP // CT
    row_count = TPP // RT
    left_iota = lax.broadcasted_iota(jnp.int32, (1, CT, col_count * TILE, 1, 1), 1)
    left_pos = lax.broadcasted_iota(jnp.int32, (1, CT, col_count * TILE, 1, 1), 2)
    right_iota = lax.broadcasted_iota(jnp.int32, (1, 1, 1, RT, row_count * TILE), 3)
    right_pos = lax.broadcasted_iota(jnp.int32, (1, 1, 1, RT, row_count * TILE), 4)
    left_index = (left_iota * col_count + left_pos // TILE) * TILE + left_pos % TILE
    right_index = (right_iota * row_count + right_pos // TILE) * TILE + right_pos % TILE
    layout = (NP, CT, col_count * TILE, RT, row_count * TILE)
    noise = jax.random.normal(key, layout, jnp.float32)
    upper = noise / jnp.sqrt(jnp.float32(PANEL))
    diagonal = jnp.exp(jax.random.uniform(jax.random.fold_in(key, 5), (NP, CT, col_count * TILE, 1, 1), jnp.float32, -0.6931472, 0.6931472))
    values = jnp.where(right_index > left_index, upper, jnp.where(right_index == left_index, diagonal, 0.0))
    return values.astype(jnp.bfloat16)


def single_permutation(subkey):
    return jax.random.permutation(subkey, NLOC)


def draw_owner_map(key, part):
    col_count = TPP // CT
    subkeys = jax.random.split(jax.random.fold_in(key, 17), col_count)
    orders = jax.vmap(single_permutation)(subkeys)
    return orders.T.astype(jnp.int32)


def draw_test_rows(key, part):
    groups = NTEST // TEST_DEV
    picks = jax.random.randint(jax.random.fold_in(key, 19), (groups, TEST_DEV), 0, POOL_DEV)
    picks = picks.at[:, 0].set(0).at[:, 1].set(POOL_DEV - 1)
    offsets = jnp.arange(groups, dtype=jnp.int32)[:, None] * POOL_DEV
    return (picks + offsets).reshape(NTEST).astype(jnp.int32)


def shard_levels(stream_key, shape, pieces, low, high):
    def one(position, shards_of):
        draws = jax.random.uniform(jax.random.fold_in(jax.random.fold_in(stream_key, 6), position), (shards_of,), jnp.float32, low / len(pieces), high / len(pieces))
        return jnp.repeat(jnp.exp(draws), shape[position] // shards_of).reshape((-1,) + (1,) * (len(shape) - position - 1))

    gain = one(*pieces[0])
    for cut in pieces[1:]:
        gain = gain * one(*cut)
    return gain


def bell_draw(key, shape, scale, limit, cuts=(), kind=jnp.bfloat16):
    values = jax.random.normal(key, shape, jnp.float32) * scale
    if len(cuts) > 0:
        values = shard_levels(key, shape, cuts, -0.22, 0.18) * values
    return jnp.clip(values, min=-limit, max=limit).astype(kind)


def setup_inputs(seed: int = 0) -> dict:
    key_of = jax.random.split(jax.random.key(seed), 8)
    factor_blocks = bell_draw(key_of[0], (PAIRS, RT, N_ROW * TILE, CT, N_COL * TILE), (4 * PANEL) ** -0.5, 0.03125, ((2, 8), (4, 16)))
    inverse_blocks = draw_inverse_blocks(jax.random.fold_in(key_of[7], 71), 0)
    right_side = bell_draw(key_of[2], (NP, RT, N_ROW * TILE, OUT), 0.25, 4.0, ((2, 8),))
    centers = draw_centers(jax.random.fold_in(key_of[7], 71), 0)
    owner_map = draw_owner_map(jax.random.fold_in(key_of[7], 71), 0)
    test_pool = draw_test_pool(jax.random.fold_in(key_of[7], 71), 0)
    test_rows = draw_test_rows(jax.random.fold_in(key_of[7], 71), 0)
    return dict(factor_blocks=factor_blocks, inverse_blocks=inverse_blocks, right_side=right_side, centers=centers, owner_map=owner_map, test_pool=test_pool, test_rows=test_rows)


inverse_width = 0.35


def pair_slot(early, successor):
    return successor * (successor - 1) // 2 + early


def reference(factor_blocks, inverse_blocks, right_side, centers, owner_map, test_pool, test_rows):
    pair_blocks = factor_blocks.reshape(PAIRS, PANEL, PANEL)
    inverse = inverse_blocks.reshape(NP, PANEL, PANEL)
    targets = right_side.reshape(NP, PANEL, OUT).astype(jnp.float32)
    solved = [None] * NP
    rounded = [None] * NP
    for current in range(NP - 1, -1, -1):
        summed = jnp.zeros((PANEL, OUT), jnp.float32)
        for successor in range(current + 1, NP):
            summed = summed + jnp.dot(pair_blocks[pair_slot(current, successor)], rounded[successor], preferred_element_type=jnp.float32)
        residue = (targets[current] - summed).astype(jnp.bfloat16)
        solved[current] = jnp.dot(inverse[current], residue, preferred_element_type=jnp.float32)
        rounded[current] = solved[current].astype(jnp.bfloat16)
    coefficient = jnp.stack(rounded).reshape(NLOC, N_COL, TILE, OUT)
    picks = jnp.broadcast_to(owner_map[:, :, None, None], (NLOC, N_COL, TILE, OUT))
    paired = jnp.take_along_axis(coefficient, picks, axis=0).reshape(NLOC * N_COL * TILE, OUT)
    span_rows = jnp.take(test_pool, test_rows, axis=0)
    flat_centers = centers.reshape(NLOC * N_COL * TILE, DIM)
    center_sq = jnp.sum(jnp.square(flat_centers.astype(jnp.float32)), axis=1)
    height = min(512, NTEST)

    def scoring(block_rows):
        block_sq = jnp.sum(jnp.square(block_rows.astype(jnp.float32)), axis=1)
        crossed = jnp.dot(block_rows, flat_centers.T, preferred_element_type=jnp.float32)
        distance = block_sq[:, None] + center_sq[None, :] - 2.0 * crossed
        kernel = jnp.exp(-inverse_width * distance).astype(jnp.bfloat16)
        return jnp.dot(kernel, paired, preferred_element_type=jnp.float32)

    estimate = lax.map(scoring, span_rows.reshape(NTEST // height, height, DIM)).reshape(NTEST, OUT)
    alpha = jnp.stack(solved).reshape(NP, CT, N_COL * TILE, OUT)
    return alpha, estimate
```

```python
import functools

import jax
import jax.numpy as jnp
from jax import lax
from jax.experimental import pallas as pl
from jax.experimental.pallas import tpu as pltpu
from jax.sharding import PartitionSpec as P

MESH = pl.DeviceIdType.MESH
F32 = jnp.float32
BF16 = jnp.bfloat16
SLOPE = -0.35 * 1.4426950408889634
ROWS_ITEM = 256


def kernel(
    owner, rows, f_hbm, d_hbm, b_hbm, cen_hbm, pool_hbm,
    alpha, pred,
    f_raw, d_raw, f_mat, d_mat, tmp32, y_buf, b_buf, cen, csq, pool_in, pool32,
    stage32, k_mat, x_buf, p32, p_send, r1_buf, r2_buf, q32, acc_f, q_send, c1_buf, h_send,
    c2_buf, acc, fs, fr, gs, gr,
    load_sem, pool_sem, r1s, r1r, r2s, r2r, c1s, c1r, c2s, c2r, c3s, c3r, fws, fwr, f1s, f1r, f2s, f2r,
):
    row = lax.axis_index("row")
    col = lax.axis_index("col")
    ry, rz = row // 2, row % 2
    pos, core = col // 2, col % 2
    partner = pos * 2 + (1 - core)
    pool_rows = pool32.shape[0]

    def load(src, dst, n):
        return pltpu.make_async_copy(src, dst, load_sem.at[n])

    loads = {}
    loads["d3"] = load(d_hbm.at[3], d_raw.at[3], 0)
    loads["y3"] = load(b_hbm.at[3], y_buf.at[3], 1)
    loads["f5"] = load(f_hbm.at[5], f_raw.at[5], 2)
    loads["d2"] = load(d_hbm.at[2], d_raw.at[2], 3)
    loads["b"] = load(b_hbm.at[pl.ds(0, 3)], b_buf, 4)
    loads["cen"] = load(cen_hbm, cen, 5)
    for n in loads:
        loads[n].start()

    def pool_copy(n):
        return pltpu.make_async_copy(
            pool_hbm.at[pl.ds(n * 1024, 1024)], pool_in.at[n % 2], pool_sem.at[n % 2]
        )

    pool_copy(0).start()
    pool_copy(1).start()
    loads["d01"] = load(d_hbm.at[pl.ds(0, 2)], d_raw.at[pl.ds(0, 2)], 6)
    loads["f04"] = load(f_hbm.at[pl.ds(0, 5)], f_raw.at[pl.ds(0, 5)], 7)
    loads["d01"].start()
    loads["f04"].start()

    barrier = pltpu.get_barrier_semaphore()
    for d in range(1, 8):
        pl.semaphore_signal(barrier, inc=1, device_id=((row + d) % 8, col), device_id_type=MESH)
        pl.semaphore_signal(barrier, inc=1, device_id=(row, (col + 2 * d) % 16), device_id_type=MESH)
    pl.semaphore_signal(barrier, inc=1, device_id=(row, partner), device_id_type=MESH)
    pl.semaphore_wait(barrier, 15)

    def relayout_d(k):
        for t in range(2):
            for h in range(2):
                v = d_raw[k, t, h * 128 : (h + 1) * 128].reshape(512, 256).astype(F32)
                for u in range(2):
                    tmp32[u] = v[:, u * 128 : (u + 1) * 128]
                    for s in range(4):
                        lane = s * 256 + u * 128
                        d_mat[t * 256 + h * 128 : t * 256 + (h + 1) * 128, lane : lane + 128] = (
                            tmp32[u, pl.ds(s, 128, stride=4), :].astype(BF16)
                        )

    def relayout_f(slot):
        for t in range(4):
            v = f_raw[slot, t].reshape(512, 256).astype(F32)
            for u in range(2):
                tmp32[u] = v[:, u * 128 : (u + 1) * 128]
                for s in range(2):
                    lane = s * 256 + u * 128
                    f_mat[t * 256 : (t + 1) * 256, lane : lane + 128] = (
                        tmp32[u, pl.ds(s, 256, stride=2), :].astype(BF16)
                    )

    def pool_convert():
        for n in range(6):
            pool_copy(n).wait()

            @pl.loop(0, 16)
            def _(i):
                pool32[pl.ds(pl.multiple_of(n * 1024 + i * 64, 64), 64), :] = pool_in[
                    n % 2, pl.ds(pl.multiple_of(i * 64, 64), 64), :
                ].astype(F32)

            if n + 2 < 6:
                pool_copy(n + 2).start()

    def center_tile(p):
        which = jnp.int32(0)
        for l in range(1, 8):
            which = jnp.where(owner[l] == p, l, which)
        return which

    def center_squares():
        for p in range(8):
            v = cen[p].astype(F32)
            s = jnp.sum(v * v, axis=1, keepdims=True) * SLOPE
            csq[p] = jnp.transpose(jnp.broadcast_to(s, (256, 128)))[0:8, :]

    def score_item(n):
        base = pl.multiple_of(n * ROWS_ITEM, ROWS_ITEM)

        @pl.loop(0, ROWS_ITEM // 8)
        def _(i):
            for j in range(8):
                at = jnp.maximum(rows[base + i * 8 + j] - row * pool_rows, 0)
                stage32[pl.ds(i * 8 + j, 1), :] = pool32[pl.ds(at, 1), :]

        v = stage32[...]
        ssq = jnp.sum(v * v, axis=1, keepdims=True) * SLOPE
        vb = v.astype(BF16)

        @pl.loop(0, 4)
        def _(kk):
            for t in range(2):
                which = center_tile(kk * 2 + t)
                cross = lax.dot_general(
                    vb, cen[which], (((1,), (1,)), ((), ())), preferred_element_type=F32
                )
                e = (cross * (-2.0 * SLOPE) + ssq) + csq[which][0:1, :]
                k_mat[kk, pl.ds(base, ROWS_ITEM), t * 256 : (t + 1) * 256] = jnp.exp2(e).astype(BF16)

    loads["d3"].wait()
    loads["y3"].wait()
    relayout_d(3)
    for n in ("f5", "d2", "b", "cen", "d01", "f04"):
        loads[n].wait()
    pool_convert()
    center_squares()

    @pl.loop(0, 16)
    def _(n):
        score_item(n)

    @pl.loop(0, 4)
    def _(i):
        k = 3 - i
        part = jnp.dot(d_mat[...], y_buf[k].reshape(1024, 128), preferred_element_type=F32)
        p32[...] = part
        p_send[k] = part.astype(BF16)
        r1 = []
        for d in range(1, 4):
            to = (ry + d) % 4
            r1.append(pltpu.make_async_remote_copy(
                p_send.at[k, pl.ds(pl.multiple_of(to * 128, 128), 128)], r1_buf.at[k, ry],
                r1s.at[k, d], r1r.at[k, ry], device_id=(to * 2 + rz, col), device_id_type=MESH))
        for c in r1:
            c.start()

        @pl.when(k > 0)
        def _():
            relayout_f(jnp.maximum(k * (k - 1) // 2 + k - 1, 0))

        total = p32[pl.ds(pl.multiple_of(ry * 128, 128), 128), :]
        for d in range(1, 4):
            other = (ry + d) % 4
            pltpu.make_async_remote_copy(
                p_send.at[k, pl.ds(0, 128)], r1_buf.at[k, other],
                r1s.at[k, d], r1r.at[k, other], device_id=(row, col), device_id_type=MESH).wait_recv()
            total = total + r1_buf[k, other].astype(F32)
        r2_buf[k, row] = total.astype(BF16)
        r2 = []
        for d in range(1, 8):
            r2.append(pltpu.make_async_remote_copy(
                r2_buf.at[k, row], r2_buf.at[k, row],
                r2s.at[k, d], r2r.at[k, row], device_id=((row + d) % 8, col), device_id_type=MESH))
        for c in r2:
            c.start()
        for c in r1:
            c.wait_send()

        acc_f[...] = jnp.zeros_like(acc_f)

        for d in range(1, 8):
            other = (row + d) % 8
            pltpu.make_async_remote_copy(
                r2_buf.at[k, other], r2_buf.at[k, other],
                r2s.at[k, d], r2r.at[k, other], device_id=(row, col), device_id_type=MESH).wait_recv()
        for q in range(4):
            xq = r2_buf[k, 2 * q].astype(F32) + r2_buf[k, 2 * q + 1].astype(F32)
            alpha[k, q // 2, (q % 2) * 128 : (q % 2 + 1) * 128, :] = xq
            x_buf[k, q * 128 : (q + 1) * 128, :] = xq.astype(BF16)
        for c in r2:
            c.wait_send()

        @pl.when(k > 0)
        def _():
            prod = jnp.dot(f_mat[...], x_buf[k], preferred_element_type=F32)
            q32[...] = prod

            @pl.loop(k + 1, 4)
            def _(l):
                relayout_f(l * (l - 1) // 2 + k - 1)
                q32[...] += jnp.dot(f_mat[...], x_buf[l], preferred_element_type=F32)

            q_send[k] = q32[pl.ds(pl.multiple_of((1 - core) * 512, 512), 512), :].astype(BF16)
            c1 = pltpu.make_async_remote_copy(
                q_send.at[k], c1_buf.at[k], c1s.at[k], c1r.at[k],
                device_id=(row, partner), device_id_type=MESH)
            c1.start()
            c1.wait_recv()
            half = q32[pl.ds(pl.multiple_of(core * 512, 512), 512), :] + c1_buf[k].astype(F32)
            h_send[k] = half.astype(BF16)
            p32[...] = half
            c2 = []
            for d in range(1, 8):
                to = (pos + d) % 8
                c2.append(pltpu.make_async_remote_copy(
                    h_send.at[k, pl.ds(pl.multiple_of(to * 64, 64), 64)], c2_buf.at[k, pos],
                    c2s.at[k, d], c2r.at[k, pos], device_id=(row, to * 2 + core), device_id_type=MESH))
            for c in c2:
                c.start()
            c1.wait_send()
            relayout_d(k - 1)
            s = p32[pl.ds(pl.multiple_of(pos * 64, 64), 64), :]
            for d in range(1, 8):
                other = (pos + d) % 8
                pltpu.make_async_remote_copy(
                    h_send.at[k, pl.ds(0, 64)], c2_buf.at[k, other],
                    c2s.at[k, d], c2r.at[k, other], device_id=(row, col), device_id_type=MESH).wait_recv()
                s = s + c2_buf[k, other].astype(F32)
            own = pl.multiple_of(core * 512 + pos * 64, 64)
            mine_t, mine_a = own // 256, pl.multiple_of(own % 256, 64)
            target = b_buf[k - 1, mine_t, pl.ds(mine_a, 64), :].astype(F32)
            y_buf[k - 1, mine_t, pl.ds(mine_a, 64), :] = (target - s).astype(BF16)

            def y_at(half_of, p):
                o = half_of * 512 + p * 64
                return y_buf.at[k - 1, o // 256, pl.ds(pl.multiple_of(o % 256, 64), 64)]

            c3 = []
            for d in range(1, 8):
                c3.append(pltpu.make_async_remote_copy(
                    y_at(core, pos), y_at(core, pos), c3s.at[k, d], c3r.at[k, pos],
                    device_id=(row, (pos + d) % 8 * 2 + core), device_id_type=MESH))
            fw = [pltpu.make_async_remote_copy(
                y_at(core, pos), y_at(core, pos), fws.at[k, 0], fwr.at[k, pos],
                device_id=(row, partner), device_id_type=MESH)]
            for c in c3:
                c.start()
            fw[0].start()
            for c in c2:
                c.wait_send()
            for d in range(1, 8):
                other = (pos + d) % 8
                pltpu.make_async_remote_copy(
                    y_at(core, other), y_at(core, other), c3s.at[k, d], c3r.at[k, other],
                    device_id=(row, col), device_id_type=MESH).wait_recv()
                c = pltpu.make_async_remote_copy(
                    y_at(core, other), y_at(core, other), fws.at[k, d], fwr.at[k, other],
                    device_id=(row, partner), device_id_type=MESH)
                c.start()
                fw.append(c)
            for d in range(8):
                other = (pos + d) % 8
                pltpu.make_async_remote_copy(
                    y_at(1 - core, other), y_at(1 - core, other), fws.at[k, d], fwr.at[k, other],
                    device_id=(row, col), device_id_type=MESH).wait_recv()
            for c in c3 + fw:
                c.wait_send()

    @pl.loop(0, 16)
    def _(n):
        at = pl.ds(pl.multiple_of(n * 256, 256), 256)
        v = jnp.dot(k_mat[3, at, :], x_buf[3], preferred_element_type=F32)
        for kk in (2, 1):
            v = v + jnp.dot(k_mat[kk, at, :], x_buf[kk], preferred_element_type=F32)
        acc[at, :] = v

    def last(chunk):
        at = pl.ds(pl.multiple_of(chunk * 256, 256), 256)
        return acc[at, :] + jnp.dot(k_mat[0, at, :], x_buf[0], preferred_element_type=F32)

    def to_partner(p):
        return pltpu.make_async_remote_copy(
            fs.at[p], fr.at[p], f1s.at[p], f1r.at[p], device_id=(row, partner), device_id_type=MESH)

    def to_owner(p):
        return pltpu.make_async_remote_copy(
            gs.at[p], gr.at[pos], f2s.at[p], f2r.at[pos], device_id=(row, p * 2 + core), device_id_type=MESH)

    @pl.loop(1, 9)
    def _(d):
        p = (pos + d) % 8
        fs[p] = last(p * 2 + 1 - core).astype(BF16)
        to_partner(p).start()

    @pl.loop(1, 8)
    def _(d):
        p = (pos + d) % 8
        v = last(p * 2 + core)
        to_partner(p).wait_recv()
        gs[p] = (v + fr[p].astype(F32)).astype(BF16)
        to_owner(p).start()

    v = last(pos * 2 + core)
    to_partner(pos).wait_recv()
    v = v + fr[pos].astype(F32)
    for d in range(1, 8):
        other = (pos + d) % 8
        pltpu.make_async_remote_copy(
            gs.at[other], gr.at[other], f2s.at[other], f2r.at[other],
            device_id=(row, col), device_id_type=MESH).wait_recv()
        v = v + gr[other].astype(F32)
    pred[...] = v

    @pl.loop(1, 8)
    def _(d):
        p = (pos + d) % 8
        to_partner(p).wait_send()
        to_owner(p).wait_send()

    to_partner(pos).wait_send()


def shards(factor_blocks, inverse_blocks, right_side, centers, owner_map, test_pool, test_rows):
    any_ = pl.BlockSpec(memory_space=pl.ANY)
    smem = pl.BlockSpec(memory_space=pltpu.SMEM)
    vmem = pl.BlockSpec(memory_space=pltpu.VMEM)
    V = pltpu.VMEM
    dma = pltpu.SemaphoreType.DMA
    scratch = [
        V((6, 4, 256, 2, 256), BF16), V((4, 2, 256, 4, 256), BF16), V((1024, 512), BF16), V((512, 1024), BF16),
        V((2, 512, 128), F32), V((4, 4, 256, 128), BF16), V((3, 4, 256, 128), BF16), V((8, 256, 512), BF16),
        V((8, 8, 256), F32), V((2, 1024, 512), BF16), V((6144, 512), F32), V((ROWS_ITEM, 512), F32),
        V((4, 4096, 512), BF16), V((4, 512, 128), BF16), V((512, 128), F32), V((4, 512, 128), BF16),
        V((4, 4, 128, 128), BF16), V((4, 8, 128, 128), BF16), V((1024, 128), F32), V((8, 128), F32),
        V((4, 512, 128), BF16), V((4, 512, 128), BF16), V((4, 512, 128), BF16), V((4, 8, 64, 128), BF16),
        V((4096, 128), F32), V((8, 256, 128), BF16), V((8, 256, 128), BF16), V((8, 256, 128), BF16),
        V((8, 256, 128), BF16),
        dma((8,)), dma((2,)), dma((4, 4)), dma((4, 4)), dma((4, 8)), dma((4, 8)), dma((4,)), dma((4,)),
        dma((4, 8)), dma((4, 8)), dma((4, 8)), dma((4, 8)), dma((4, 8)), dma((4, 8)),
        dma((8,)), dma((8,)), dma((8,)), dma((8,)),
    ]
    return pl.pallas_call(
        kernel,
        out_shape=(
            jax.ShapeDtypeStruct((4, 2, 256, 128), F32),
            jax.ShapeDtypeStruct((256, 128), F32),
        ),
        in_specs=[smem, smem, any_, any_, any_, any_, any_],
        out_specs=(vmem, vmem),
        scratch_shapes=scratch,
        name="solve_and_score",
        compiler_params=pltpu.CompilerParams(
            collective_id=0, has_side_effects=True, vmem_limit_bytes=67043328
        ),
    )(owner_map.reshape(8), test_rows, factor_blocks, inverse_blocks, right_side, centers, test_pool)


def solution(mesh):
    in_specs = (
        P(None, None, "row", None, "col"),
        P(None, None, "col", None, "row"),
        P(None, None, "row", None),
        P(None, "col", None),
        P(None, "col"),
        P("row", None),
        P("row"),
    )
    out_specs = (P(None, None, "col", None), P(("row", "col"), None))
    return jax.shard_map(shards, mesh=mesh, in_specs=in_specs, out_specs=out_specs, check_vma=False)
```

```python
import functools

import jax
import jax.numpy as jnp
from jax import lax
from jax.experimental import pallas as pl
from jax.experimental.pallas import tpu as pltpu
from jax.sharding import PartitionSpec as P

MESH = pl.DeviceIdType.MESH
F32 = jnp.float32
BF16 = jnp.bfloat16
SLOPE = -0.35 * 1.4426950408889634
ROWS_ITEM = 512
GATHERS = ((0, 0, 1, 1), (0, 1, 1, 1), (0, 1, 0, 1), (1, 0, 0, 0))
PIECES = ((0, 0, 2, 4), (2, 4, 2, 4), (2, 2, 2, 4), (1, 3, 0, 0))


def starts(plan):
    out, done = [], 0
    for counts in plan:
        out.append([])
        for count in counts:
            out[-1].append(done)
            done += count
    return out, done


def at_step(i, values):
    d = list(values)
    steps = []
    while d:
        steps.append(d[0])
        d = [d[n + 1] - d[n] for n in range(len(d) - 1)]
    pair = lax.div(i * (i - 1), 2)
    triple = lax.div(i * (i - 1) * (i - 2), 6)
    return steps[0] + steps[1] * i + steps[2] * pair + steps[3] * triple


def kernel(
    owner, rows, f_hbm, d_hbm, b_hbm, cen_hbm, pool_hbm,
    alpha, pred,
    f_raw, d_raw, f_mat, d_mat, tmp32, y_buf, b_buf, cen, csq, pool_in, pool4,
    stage4, span, ssq, k_mat, x_buf, p32, p_send, r1_buf, r2_buf, q32, acc_f, q_send, c1_buf, h_send,
    c2_buf, acc, fs, fr, gs, gr,
    load_sem, pool_sem, r1s, r1r, r2s, r2r, c1s, c1r, c2s, c2r, c3s, c3r, fws, fwr, f1s, f1r, f2s, f2r,
):
    row = lax.axis_index("row")
    col = lax.axis_index("col")
    ry, rz = row // 2, row % 2
    pos, core = col // 2, col % 2
    partner = pos * 2 + (1 - core)
    pool_rows = pool4.shape[0] // 4

    def load(src, dst, n):
        return pltpu.make_async_copy(src, dst, load_sem.at[n])

    loads = {}
    loads["d3"] = load(d_hbm.at[3], d_raw.at[3], 0)
    loads["y3"] = load(b_hbm.at[3], y_buf.at[3], 1)
    loads["f5"] = load(f_hbm.at[5], f_raw.at[5], 2)
    loads["d2"] = load(d_hbm.at[2], d_raw.at[2], 3)
    loads["b"] = load(b_hbm.at[pl.ds(0, 3)], b_buf, 4)
    loads["cen"] = load(cen_hbm, cen, 5)
    for n in loads:
        loads[n].start()

    def pool_copy(n):
        return pltpu.make_async_copy(
            pool_hbm.at[pl.ds(n * 1024, 1024)], pool_in.at[n % 2], pool_sem.at[n % 2]
        )

    pool_copy(0).start()
    pool_copy(1).start()
    loads["d01"] = load(d_hbm.at[pl.ds(0, 2)], d_raw.at[pl.ds(0, 2)], 6)
    loads["f04"] = load(f_hbm.at[pl.ds(0, 5)], f_raw.at[pl.ds(0, 5)], 7)
    loads["d01"].start()
    loads["f04"].start()

    barrier = pltpu.get_barrier_semaphore()
    for d in range(1, 8):
        pl.semaphore_signal(barrier, inc=1, device_id=((row + d) % 8, col), device_id_type=MESH)
        pl.semaphore_signal(barrier, inc=1, device_id=(row, (col + 2 * d) % 16), device_id_type=MESH)
    pl.semaphore_signal(barrier, inc=1, device_id=(row, partner), device_id_type=MESH)

    def relayout_d(k):
        for t in range(2):
            for h in range(2):
                v = d_raw[k, t, h * 128 : (h + 1) * 128].reshape(512, 256).astype(F32)
                for u in range(2):
                    tmp32[u] = v[:, u * 128 : (u + 1) * 128]
                    for s in range(4):
                        lane = s * 256 + u * 128
                        d_mat[t * 256 + h * 128 : t * 256 + (h + 1) * 128, lane : lane + 128] = (
                            tmp32[u, pl.ds(s, 128, stride=4), :].astype(BF16)
                        )

    def relayout_f(slot):
        for t in range(4):
            v = f_raw[slot, t].reshape(512, 256).astype(F32)
            for u in range(2):
                tmp32[u] = v[:, u * 128 : (u + 1) * 128]
                for s in range(2):
                    lane = s * 256 + u * 128
                    f_mat[t * 256 : (t + 1) * 256, lane : lane + 128] = (
                        tmp32[u, pl.ds(s, 256, stride=2), :].astype(BF16)
                    )

    def pool_convert():
        for n in range(6):
            pool_copy(n).wait()

            @pl.loop(0, 16)
            def _(i):
                v = pool_in[n % 2, pl.ds(pl.multiple_of(i * 64, 64), 64), :].astype(F32)
                for q in range(4):
                    at = pl.multiple_of(n * 4096 + i * 256, 256)
                    pool4[pl.ds(at + q, 64, stride=4), :] = v[:, q * 128 : (q + 1) * 128]

            if n + 2 < 6:
                pool_copy(n + 2).start()

    def center_tile(p):
        which = jnp.int32(0)
        for l in range(1, 8):
            which = jnp.where(owner[l] == p, l, which)
        return which

    def center_squares():
        for p in range(8):
            v = cen[p].astype(F32)
            s = jnp.sum(v * v, axis=1, keepdims=True) * SLOPE
            csq[p] = jnp.transpose(jnp.broadcast_to(s, (256, 128)))[0:8, :]

    def gather_item(n):
        base = pl.multiple_of(n * ROWS_ITEM, ROWS_ITEM)

        @pl.loop(0, ROWS_ITEM // 16)
        def _(i):
            for j in range(16):
                at = jnp.maximum(rows[base + i * 16 + j] - row * pool_rows, 0)
                stage4[pl.ds(pl.multiple_of((i * 16 + j) * 4, 4), 4), :] = pool4[
                    pl.ds(at * 4, 4), :
                ]

        slot = lax.rem(n, 2)
        total = None
        for q in range(4):
            v = stage4[pl.ds(q, ROWS_ITEM, stride=4), :]
            span[slot, :, q * 128 : (q + 1) * 128] = v.astype(BF16)
            total = v * v if total is None else total + v * v
        total = jnp.sum(total, axis=1, keepdims=True) * SLOPE
        ssq[slot] = jnp.broadcast_to(total, (ROWS_ITEM, 128))

    def score_item(n, kk):
        slot = lax.rem(n, 2)
        base = pl.multiple_of(n * ROWS_ITEM, ROWS_ITEM)
        for t in range(2):
            which = center_tile(kk * 2 + t)
            cross = lax.dot_general(
                span[slot], cen[which], (((1,), (1,)), ((), ())), preferred_element_type=F32
            )
            for u in range(2):
                lanes = slice(u * 128, (u + 1) * 128)
                e = (cross[:, lanes] * (-2.0 * SLOPE) + ssq[slot]) + csq[which][0:1, lanes]
                k_mat[kk, pl.ds(base, ROWS_ITEM), t * 256 + u * 128 : t * 256 + (u + 1) * 128] = (
                    jnp.exp2(e).astype(BF16)
                )

    gather_at, gathers = starts(GATHERS)
    piece_at, pieces = starts(PIECES)
    assert gathers * ROWS_ITEM == k_mat.shape[1] and pieces == 4 * gathers

    def score_work(i, site):
        first = at_step(i, [at[site] for at in gather_at])

        @pl.loop(first, first + at_step(i, [panel[site] for panel in GATHERS]))
        def _(n):
            gather_item(n)

        first = at_step(i, [at[site] for at in piece_at])

        @pl.loop(first, first + at_step(i, [panel[site] for panel in PIECES]))
        def _(u):
            n = lax.div(u, 4)
            score_item(n, u - n * 4)

    loads["d3"].wait()
    loads["y3"].wait()
    relayout_d(3)
    @pl.loop(0, 4)
    def _(i):
        k = 3 - i
        part = jnp.dot(d_mat[...], y_buf[k].reshape(1024, 128), preferred_element_type=F32)
        p32[...] = part
        p_send[k] = part.astype(BF16)

        @pl.when(i == 0)
        def _():
            pl.semaphore_wait(barrier, 15)

        r1 = []
        for d in range(1, 4):
            to = (ry + d) % 4
            r1.append(pltpu.make_async_remote_copy(
                p_send.at[k, pl.ds(pl.multiple_of(to * 128, 128), 128)], r1_buf.at[k, ry],
                r1s.at[k, d], r1r.at[k, ry], device_id=(to * 2 + rz, col), device_id_type=MESH))
        for c in r1:
            c.start()

        score_work(i, 0)

        total = p32[pl.ds(pl.multiple_of(ry * 128, 128), 128), :]
        for d in range(1, 4):
            other = (ry + d) % 4
            pltpu.make_async_remote_copy(
                p_send.at[k, pl.ds(0, 128)], r1_buf.at[k, other],
                r1s.at[k, d], r1r.at[k, other], device_id=(row, col), device_id_type=MESH).wait_recv()
            total = total + r1_buf[k, other].astype(F32)
        r2_buf[k, row] = total.astype(BF16)
        r2 = []
        for d in range(1, 8):
            r2.append(pltpu.make_async_remote_copy(
                r2_buf.at[k, row], r2_buf.at[k, row],
                r2s.at[k, d], r2r.at[k, row], device_id=((row + d) % 8, col), device_id_type=MESH))
        for c in r2:
            c.start()
        for c in r1:
            c.wait_send()

        @pl.when(i == 0)
        def _():
            loads["f5"].wait()
            loads["cen"].wait()
            center_squares()

        @pl.when(k > 0)
        def _():
            q32[...] = jnp.zeros_like(q32)

            @pl.loop(k + 1, 4)
            def _(l):
                relayout_f(l * (l - 1) // 2 + k - 1)
                q32[...] += jnp.dot(f_mat[...], x_buf[l], preferred_element_type=F32)

            relayout_f(k * (k - 1) // 2 + k - 1)

        @pl.when(i == 0)
        def _():
            pool_convert()

        score_work(i, 1)

        @pl.when(k == 0)
        def _():
            @pl.loop(0, 16)
            def _(n):
                at = pl.ds(pl.multiple_of(n * 256, 256), 256)
                v = jnp.dot(k_mat[3, at, :], x_buf[3], preferred_element_type=F32)
                for kk in (2, 1):
                    v = v + jnp.dot(k_mat[kk, at, :], x_buf[kk], preferred_element_type=F32)
                acc[at, :] = v

        for d in range(1, 8):
            other = (row + d) % 8
            pltpu.make_async_remote_copy(
                r2_buf.at[k, other], r2_buf.at[k, other],
                r2s.at[k, d], r2r.at[k, other], device_id=(row, col), device_id_type=MESH).wait_recv()
        for q in range(4):
            xq = r2_buf[k, 2 * q].astype(F32) + r2_buf[k, 2 * q + 1].astype(F32)
            alpha[k, q // 2, (q % 2) * 128 : (q % 2 + 1) * 128, :] = xq
            x_buf[k, q * 128 : (q + 1) * 128, :] = xq.astype(BF16)
        for c in r2:
            c.wait_send()

        @pl.when(k > 0)
        def _():
            q32[...] += jnp.dot(f_mat[...], x_buf[k], preferred_element_type=F32)
            q_send[k] = q32[pl.ds(pl.multiple_of((1 - core) * 512, 512), 512), :].astype(BF16)
            c1 = pltpu.make_async_remote_copy(
                q_send.at[k], c1_buf.at[k], c1s.at[k], c1r.at[k],
                device_id=(row, partner), device_id_type=MESH)
            c1.start()
            c1.wait_recv()
            half = q32[pl.ds(pl.multiple_of(core * 512, 512), 512), :] + c1_buf[k].astype(F32)
            h_send[k] = half.astype(BF16)
            p32[...] = half
            c2 = []
            for d in range(1, 8):
                to = (pos + d) % 8
                c2.append(pltpu.make_async_remote_copy(
                    h_send.at[k, pl.ds(pl.multiple_of(to * 64, 64), 64)], c2_buf.at[k, pos],
                    c2s.at[k, d], c2r.at[k, pos], device_id=(row, to * 2 + core), device_id_type=MESH))
            for c in c2:
                c.start()
            c1.wait_send()

            @pl.when(i == 0)
            def _():
                loads["d2"].wait()
                loads["b"].wait()

            relayout_d(k - 1)
            score_work(i, 2)
            s = p32[pl.ds(pl.multiple_of(pos * 64, 64), 64), :]
            for d in range(1, 8):
                other = (pos + d) % 8
                pltpu.make_async_remote_copy(
                    h_send.at[k, pl.ds(0, 64)], c2_buf.at[k, other],
                    c2s.at[k, d], c2r.at[k, other], device_id=(row, col), device_id_type=MESH).wait_recv()
                s = s + c2_buf[k, other].astype(F32)
            own = pl.multiple_of(core * 512 + pos * 64, 64)
            mine_t, mine_a = own // 256, pl.multiple_of(own % 256, 64)
            target = b_buf[k - 1, mine_t, pl.ds(mine_a, 64), :].astype(F32)
            y_buf[k - 1, mine_t, pl.ds(mine_a, 64), :] = (target - s).astype(BF16)

            def y_at(half_of, p):
                o = half_of * 512 + p * 64
                return y_buf.at[k - 1, o // 256, pl.ds(pl.multiple_of(o % 256, 64), 64)]

            c3 = []
            for d in range(1, 8):
                c3.append(pltpu.make_async_remote_copy(
                    y_at(core, pos), y_at(core, pos), c3s.at[k, d], c3r.at[k, pos],
                    device_id=(row, (pos + d) % 8 * 2 + core), device_id_type=MESH))
            fw = [pltpu.make_async_remote_copy(
                y_at(core, pos), y_at(core, pos), fws.at[k, 0], fwr.at[k, pos],
                device_id=(row, partner), device_id_type=MESH)]
            for c in c3:
                c.start()
            fw[0].start()
            for c in c2:
                c.wait_send()

            @pl.when(i == 0)
            def _():
                loads["d01"].wait()
                loads["f04"].wait()

            score_work(i, 3)
            for d in range(1, 8):
                other = (pos + d) % 8
                pltpu.make_async_remote_copy(
                    y_at(core, other), y_at(core, other), c3s.at[k, d], c3r.at[k, other],
                    device_id=(row, col), device_id_type=MESH).wait_recv()
                c = pltpu.make_async_remote_copy(
                    y_at(core, other), y_at(core, other), fws.at[k, d], fwr.at[k, other],
                    device_id=(row, partner), device_id_type=MESH)
                c.start()
                fw.append(c)
            for d in range(8):
                other = (pos + d) % 8
                pltpu.make_async_remote_copy(
                    y_at(1 - core, other), y_at(1 - core, other), fws.at[k, d], fwr.at[k, other],
                    device_id=(row, col), device_id_type=MESH).wait_recv()
            for c in c3 + fw:
                c.wait_send()

    def last(chunk):
        at = pl.ds(pl.multiple_of(chunk * 256, 256), 256)
        return acc[at, :] + jnp.dot(k_mat[0, at, :], x_buf[0], preferred_element_type=F32)

    def to_partner(p):
        return pltpu.make_async_remote_copy(
            fs.at[p], fr.at[p], f1s.at[p], f1r.at[p], device_id=(row, partner), device_id_type=MESH)

    def to_owner(p):
        return pltpu.make_async_remote_copy(
            gs.at[p], gr.at[pos], f2s.at[p], f2r.at[pos], device_id=(row, p * 2 + core), device_id_type=MESH)

    @pl.loop(1, 9)
    def _(d):
        p = (pos + d) % 8
        fs[p] = last(p * 2 + 1 - core).astype(BF16)
        to_partner(p).start()

    @pl.loop(1, 8)
    def _(d):
        p = (pos + d) % 8
        v = last(p * 2 + core)
        to_partner(p).wait_recv()
        gs[p] = (v + fr[p].astype(F32)).astype(BF16)
        to_owner(p).start()

    v = last(pos * 2 + core)
    to_partner(pos).wait_recv()
    v = v + fr[pos].astype(F32)
    for d in range(1, 8):
        other = (pos + d) % 8
        pltpu.make_async_remote_copy(
            gs.at[other], gr.at[other], f2s.at[other], f2r.at[other],
            device_id=(row, col), device_id_type=MESH).wait_recv()
        v = v + gr[other].astype(F32)
    pred[...] = v

    @pl.loop(1, 8)
    def _(d):
        p = (pos + d) % 8
        to_partner(p).wait_send()
        to_owner(p).wait_send()

    to_partner(pos).wait_send()


def shards(factor_blocks, inverse_blocks, right_side, centers, owner_map, test_pool, test_rows):
    any_ = pl.BlockSpec(memory_space=pl.ANY)
    smem = pl.BlockSpec(memory_space=pltpu.SMEM)
    vmem = pl.BlockSpec(memory_space=pltpu.VMEM)
    V = pltpu.VMEM
    dma = pltpu.SemaphoreType.DMA
    scratch = [
        V((6, 4, 256, 2, 256), BF16), V((4, 2, 256, 4, 256), BF16), V((1024, 512), BF16), V((512, 1024), BF16),
        V((2, 512, 128), F32), V((4, 4, 256, 128), BF16), V((3, 4, 256, 128), BF16), V((8, 256, 512), BF16),
        V((8, 8, 256), F32), V((2, 1024, 512), BF16), V((6144 * 4, 128), F32), V((ROWS_ITEM * 4, 128), F32),
        V((2, ROWS_ITEM, 512), BF16), V((2, ROWS_ITEM, 128), F32),
        V((4, 4096, 512), BF16), V((4, 512, 128), BF16), V((512, 128), F32), V((4, 512, 128), BF16),
        V((4, 4, 128, 128), BF16), V((4, 8, 128, 128), BF16), V((1024, 128), F32), V((8, 128), F32),
        V((4, 512, 128), BF16), V((4, 512, 128), BF16), V((4, 512, 128), BF16), V((4, 8, 64, 128), BF16),
        V((4096, 128), F32), V((8, 256, 128), BF16), V((8, 256, 128), BF16), V((8, 256, 128), BF16),
        V((8, 256, 128), BF16),
        dma((8,)), dma((2,)), dma((4, 4)), dma((4, 4)), dma((4, 8)), dma((4, 8)), dma((4,)), dma((4,)),
        dma((4, 8)), dma((4, 8)), dma((4, 8)), dma((4, 8)), dma((4, 8)), dma((4, 8)),
        dma((8,)), dma((8,)), dma((8,)), dma((8,)),
    ]
    return pl.pallas_call(
        kernel,
        out_shape=(
            jax.ShapeDtypeStruct((4, 2, 256, 128), F32),
            jax.ShapeDtypeStruct((256, 128), F32),
        ),
        in_specs=[smem, smem, any_, any_, any_, any_, any_],
        out_specs=(vmem, vmem),
        scratch_shapes=scratch,
        name="solve_and_score",
        compiler_params=pltpu.CompilerParams(
            collective_id=0, has_side_effects=True, vmem_limit_bytes=67043328
        ),
    )(owner_map.reshape(8), test_rows, factor_blocks, inverse_blocks, right_side, centers, test_pool)


def solution(mesh):
    in_specs = (
        P(None, None, "row", None, "col"),
        P(None, None, "col", None, "row"),
        P(None, None, "row", None),
        P(None, "col", None),
        P(None, "col"),
        P("row", None),
        P("row"),
    )
    out_specs = (P(None, None, "col", None), P(("row", "col"), None))
    return jax.shard_map(shards, mesh=mesh, in_specs=in_specs, out_specs=out_specs, check_vma=False)
```

```python
import functools

import jax
import jax.numpy as jnp
from jax import lax
from jax.experimental import pallas as pl
from jax.experimental.pallas import tpu as pltpu
from jax.sharding import PartitionSpec as P

MESH = pl.DeviceIdType.MESH
F32 = jnp.float32
BF16 = jnp.bfloat16
SLOPE = -0.35 * 1.4426950408889634
ROWS_ITEM = 512
GATHERS = ((0, 0, 1, 1), (0, 1, 1, 1), (0, 1, 0, 1), (1, 0, 0, 0))
PIECES = ((0, 0, 2, 4), (2, 4, 2, 4), (2, 2, 2, 4), (1, 3, 0, 0))


FAR = ((2, 1), (1, 1), (3, 1), (2, 0), (1, 0), (3, 0), (0, 1))
NEAR = FAR[::-1]
ROW_FAR = ((2, 1), (1, 1), (3, 1), (0, 1), (2, 0), (1, 0), (3, 0))


def starts(plan):
    out, done = [], 0
    for counts in plan:
        out.append([])
        for count in counts:
            out[-1].append(done)
            done += count
    return out, done


def at_step(i, values):
    d = list(values)
    steps = []
    while d:
        steps.append(d[0])
        d = [d[n + 1] - d[n] for n in range(len(d) - 1)]
    pair = lax.div(i * (i - 1), 2)
    triple = lax.div(i * (i - 1) * (i - 2), 6)
    return steps[0] + steps[1] * i + steps[2] * pair + steps[3] * triple


def kernel(
    owner, rows, f_hbm, d_hbm, b_hbm, cen_hbm, pool_hbm,
    alpha, pred,
    f_raw, d_raw, f_mat, d_mat, tmp32, y_buf, b_buf, cen, csq, pool_in, pool4,
    stage4, span, ssq, k_mat, x_buf, p32, p_send, r1_buf, r2_buf, q32, acc_f, q_send, c1_buf, h_send,
    c2_buf, acc, fs, fr, gs, gr,
    load_sem, pool_sem, r1s, r1r, r2s, r2r, c1s, c1r, c2s, c2r, c3s, c3r, fws, fwr, f1s, f1r, f2s, f2r,
):
    row = lax.axis_index("row")
    col = lax.axis_index("col")
    ry, rz = row // 2, row % 2
    pos, core = col // 2, col % 2
    partner = pos * 2 + (1 - core)

    def row_at(step):
        return (ry + step[0]) % 4 * 2 + (rz + step[1]) % 2

    def pos_at(step):
        return (pos // 2 + step[0]) % 4 * 2 + (pos % 2 + step[1]) % 2

    pool_rows = pool4.shape[0] // 4

    def load(src, dst, n):
        return pltpu.make_async_copy(src, dst, load_sem.at[n])

    loads = {}
    loads["d3"] = load(d_hbm.at[3], d_raw.at[3], 0)
    loads["y3"] = load(b_hbm.at[3], y_buf.at[3], 1)
    loads["f5"] = load(f_hbm.at[5], f_raw.at[5], 2)
    loads["d2"] = load(d_hbm.at[2], d_raw.at[2], 3)
    loads["b"] = load(b_hbm.at[pl.ds(0, 3)], b_buf, 4)
    loads["cen"] = load(cen_hbm, cen, 5)
    for n in loads:
        loads[n].start()

    def pool_copy(n):
        return pltpu.make_async_copy(
            pool_hbm.at[pl.ds(n * 1024, 1024)], pool_in.at[n % 2], pool_sem.at[n % 2]
        )

    pool_copy(0).start()
    pool_copy(1).start()
    loads["d01"] = load(d_hbm.at[pl.ds(0, 2)], d_raw.at[pl.ds(0, 2)], 6)
    loads["f04"] = load(f_hbm.at[pl.ds(0, 5)], f_raw.at[pl.ds(0, 5)], 7)
    loads["d01"].start()
    loads["f04"].start()

    barrier = pltpu.get_barrier_semaphore()
    for d in range(1, 8):
        pl.semaphore_signal(barrier, inc=1, device_id=((row + d) % 8, col), device_id_type=MESH)
        pl.semaphore_signal(barrier, inc=1, device_id=(row, (col + 2 * d) % 16), device_id_type=MESH)
    pl.semaphore_signal(barrier, inc=1, device_id=(row, partner), device_id_type=MESH)

    def relayout_d(k):
        for t in range(2):
            for h in range(2):
                v = d_raw[k, t, h * 128 : (h + 1) * 128].reshape(512, 256).astype(F32)
                for u in range(2):
                    tmp32[u] = v[:, u * 128 : (u + 1) * 128]
                    for s in range(4):
                        lane = s * 256 + u * 128
                        d_mat[t * 256 + h * 128 : t * 256 + (h + 1) * 128, lane : lane + 128] = (
                            tmp32[u, pl.ds(s, 128, stride=4), :].astype(BF16)
                        )

    def relayout_f(slot):
        for t in range(4):
            v = f_raw[slot, t].reshape(512, 256).astype(F32)
            for u in range(2):
                tmp32[u] = v[:, u * 128 : (u + 1) * 128]
                for s in range(2):
                    lane = s * 256 + u * 128
                    f_mat[t * 256 : (t + 1) * 256, lane : lane + 128] = (
                        tmp32[u, pl.ds(s, 256, stride=2), :].astype(BF16)
                    )

    def pool_convert():
        for n in range(6):
            pool_copy(n).wait()

            @pl.loop(0, 16)
            def _(i):
                v = pool_in[n % 2, pl.ds(pl.multiple_of(i * 64, 64), 64), :].astype(F32)
                for q in range(4):
                    at = pl.multiple_of(n * 4096 + i * 256, 256)
                    pool4[pl.ds(at + q, 64, stride=4), :] = v[:, q * 128 : (q + 1) * 128]

            if n + 2 < 6:
                pool_copy(n + 2).start()

    def center_tile(p):
        which = jnp.int32(0)
        for l in range(1, 8):
            which = jnp.where(owner[l] == p, l, which)
        return which

    def center_squares():
        for p in range(8):
            v = cen[p].astype(F32)
            s = jnp.sum(v * v, axis=1, keepdims=True) * SLOPE
            csq[p] = jnp.transpose(jnp.broadcast_to(s, (256, 128)))[0:8, :]

    def gather_item(n):
        base = pl.multiple_of(n * ROWS_ITEM, ROWS_ITEM)

        @pl.loop(0, ROWS_ITEM // 16)
        def _(i):
            for j in range(16):
                at = jnp.maximum(rows[base + i * 16 + j] - row * pool_rows, 0)
                stage4[pl.ds(pl.multiple_of((i * 16 + j) * 4, 4), 4), :] = pool4[
                    pl.ds(at * 4, 4), :
                ]

        slot = lax.rem(n, 2)
        total = None
        for q in range(4):
            v = stage4[pl.ds(q, ROWS_ITEM, stride=4), :]
            span[slot, :, q * 128 : (q + 1) * 128] = v.astype(BF16)
            total = v * v if total is None else total + v * v
        total = jnp.sum(total, axis=1, keepdims=True) * SLOPE
        ssq[slot] = jnp.broadcast_to(total, (ROWS_ITEM, 128))

    def score_item(n, kk):
        slot = lax.rem(n, 2)
        base = pl.multiple_of(n * ROWS_ITEM, ROWS_ITEM)
        for t in range(2):
            which = center_tile(kk * 2 + t)
            cross = lax.dot_general(
                span[slot], cen[which], (((1,), (1,)), ((), ())), preferred_element_type=F32
            )
            for u in range(2):
                lanes = slice(u * 128, (u + 1) * 128)
                e = (cross[:, lanes] * (-2.0 * SLOPE) + ssq[slot]) + csq[which][0:1, lanes]
                k_mat[kk, pl.ds(base, ROWS_ITEM), t * 256 + u * 128 : t * 256 + (u + 1) * 128] = (
                    jnp.exp2(e).astype(BF16)
                )

    gather_at, gathers = starts(GATHERS)
    piece_at, pieces = starts(PIECES)
    assert gathers * ROWS_ITEM == k_mat.shape[1] and pieces == 4 * gathers

    def score_work(i, site):
        first = at_step(i, [at[site] for at in gather_at])

        @pl.loop(first, first + at_step(i, [panel[site] for panel in GATHERS]))
        def _(n):
            gather_item(n)

        first = at_step(i, [at[site] for at in piece_at])

        @pl.loop(first, first + at_step(i, [panel[site] for panel in PIECES]))
        def _(u):
            n = lax.div(u, 4)
            score_item(n, u - n * 4)

    loads["d3"].wait()
    loads["y3"].wait()
    relayout_d(3)
    @pl.loop(0, 4)
    def _(i):
        k = 3 - i
        rhs = y_buf[k].reshape(1024, 128)

        def quarter(d):
            return pl.ds(pl.multiple_of((ry + d) % 4 * 128, 128), 128)

        def pair(d, e):
            lhs = jnp.concatenate([d_mat[quarter(d), :], d_mat[quarter(e), :]], axis=0)
            return jnp.dot(lhs, rhs, preferred_element_type=F32)

        def first_exchange(d):
            return pltpu.make_async_remote_copy(
                p_send.at[k, quarter(d)], r1_buf.at[k, ry],
                r1s.at[k, d], r1r.at[k, ry], device_id=((ry + d) % 4 * 2 + rz, col), device_id_type=MESH)

        part = pair(2, 1)
        p_send[k, quarter(2), :] = part[0:128].astype(BF16)
        p_send[k, quarter(1), :] = part[128:256].astype(BF16)

        @pl.when(i == 0)
        def _():
            pl.semaphore_wait(barrier, 15)

        r1 = [first_exchange(d) for d in (2, 1, 3)]
        r1[0].start()
        r1[1].start()
        part = pair(3, 0)
        p_send[k, quarter(3), :] = part[0:128].astype(BF16)
        r1[2].start()
        p32[0:128] = part[128:256]

        score_work(i, 0)

        total = p32[0:128]
        for d in range(1, 4):
            other = (ry + d) % 4
            pltpu.make_async_remote_copy(
                p_send.at[k, pl.ds(0, 128)], r1_buf.at[k, other],
                r1s.at[k, d], r1r.at[k, other], device_id=(row, col), device_id_type=MESH).wait_recv()
            total = total + r1_buf[k, other].astype(F32)
        r2_buf[k, row] = total.astype(BF16)
        r2 = []
        for d, step in enumerate(ROW_FAR):
            r2.append(pltpu.make_async_remote_copy(
                r2_buf.at[k, row], r2_buf.at[k, row],
                r2s.at[k, d], r2r.at[k, row], device_id=(row_at(step), col), device_id_type=MESH))
        for c in r2:
            c.start()
        for c in r1:
            c.wait_send()

        @pl.when(i == 0)
        def _():
            loads["f5"].wait()
            loads["cen"].wait()
            center_squares()

        @pl.when(k > 0)
        def _():
            q32[...] = jnp.zeros_like(q32)

            @pl.loop(k + 1, 4)
            def _(l):
                relayout_f(l * (l - 1) // 2 + k - 1)
                q32[...] += jnp.dot(f_mat[...], x_buf[l], preferred_element_type=F32)

            relayout_f(k * (k - 1) // 2 + k - 1)

        @pl.when(i == 0)
        def _():
            pool_convert()

        score_work(i, 1)

        @pl.when(k == 0)
        def _():
            @pl.loop(0, 16)
            def _(n):
                at = pl.ds(pl.multiple_of(n * 256, 256), 256)
                v = jnp.dot(k_mat[3, at, :], x_buf[3], preferred_element_type=F32)
                for kk in (2, 1):
                    v = v + jnp.dot(k_mat[kk, at, :], x_buf[kk], preferred_element_type=F32)
                acc[at, :] = v

        for d in range(1, 8):
            other = (row + d) % 8
            pltpu.make_async_remote_copy(
                r2_buf.at[k, other], r2_buf.at[k, other],
                r2s.at[k, d], r2r.at[k, other], device_id=(row, col), device_id_type=MESH).wait_recv()
        for q in range(4):
            xq = r2_buf[k, 2 * q].astype(F32) + r2_buf[k, 2 * q + 1].astype(F32)
            alpha[k, q // 2, (q % 2) * 128 : (q % 2 + 1) * 128, :] = xq
            x_buf[k, q * 128 : (q + 1) * 128, :] = xq.astype(BF16)
        for c in r2:
            c.wait_send()

        @pl.when(k > 0)
        def _():
            def half_product(which):
                at = pl.ds(pl.multiple_of(which * 512, 512), 512)
                return q32[at, :] + jnp.dot(f_mat[at, :], x_buf[k], preferred_element_type=F32)

            q_send[k] = half_product(1 - core).astype(BF16)
            c1 = pltpu.make_async_remote_copy(
                q_send.at[k], c1_buf.at[k], c1s.at[k], c1r.at[k],
                device_id=(row, partner), device_id_type=MESH)
            c1.start()
            p32[...] = half_product(core)
            c1.wait_recv()
            half = p32[...] + c1_buf[k].astype(F32)
            h_send[k] = half.astype(BF16)
            p32[...] = half
            c2 = []
            for d, step in enumerate(FAR):
                to = pos_at(step)
                c2.append(pltpu.make_async_remote_copy(
                    h_send.at[k, pl.ds(pl.multiple_of(to * 64, 64), 64)], c2_buf.at[k, pos],
                    c2s.at[k, d], c2r.at[k, pos], device_id=(row, to * 2 + core), device_id_type=MESH))
            for c in c2:
                c.start()
            c1.wait_send()

            @pl.when(i == 0)
            def _():
                loads["d2"].wait()
                loads["b"].wait()

            relayout_d(k - 1)
            score_work(i, 2)
            s = p32[pl.ds(pl.multiple_of(pos * 64, 64), 64), :]
            for d in range(1, 8):
                other = (pos + d) % 8
                pltpu.make_async_remote_copy(
                    h_send.at[k, pl.ds(0, 64)], c2_buf.at[k, other],
                    c2s.at[k, d], c2r.at[k, other], device_id=(row, col), device_id_type=MESH).wait_recv()
                s = s + c2_buf[k, other].astype(F32)
            own = pl.multiple_of(core * 512 + pos * 64, 64)
            mine_t, mine_a = own // 256, pl.multiple_of(own % 256, 64)
            target = b_buf[k - 1, mine_t, pl.ds(mine_a, 64), :].astype(F32)
            y_buf[k - 1, mine_t, pl.ds(mine_a, 64), :] = (target - s).astype(BF16)

            def y_at(half_of, p):
                o = half_of * 512 + p * 64
                return y_buf.at[k - 1, o // 256, pl.ds(pl.multiple_of(o % 256, 64), 64)]

            c3 = []
            for d, step in enumerate(FAR):
                c3.append(pltpu.make_async_remote_copy(
                    y_at(core, pos), y_at(core, pos), c3s.at[k, d], c3r.at[k, pos],
                    device_id=(row, pos_at(step) * 2 + core), device_id_type=MESH))
            fw = [pltpu.make_async_remote_copy(
                y_at(core, pos), y_at(core, pos), fws.at[k, 0], fwr.at[k, pos],
                device_id=(row, partner), device_id_type=MESH)]
            for c in c3:
                c.start()
            fw[0].start()
            for c in c2:
                c.wait_send()

            @pl.when(i == 0)
            def _():
                loads["d01"].wait()
                loads["f04"].wait()

            score_work(i, 3)
            for d, step in enumerate(NEAR, 1):
                other = pos_at(step)
                pltpu.make_async_remote_copy(
                    y_at(core, other), y_at(core, other), c3s.at[k, d], c3r.at[k, other],
                    device_id=(row, col), device_id_type=MESH).wait_recv()
                c = pltpu.make_async_remote_copy(
                    y_at(core, other), y_at(core, other), fws.at[k, d], fwr.at[k, other],
                    device_id=(row, partner), device_id_type=MESH)
                c.start()
                fw.append(c)
            for d in range(8):
                other = (pos + d) % 8
                pltpu.make_async_remote_copy(
                    y_at(1 - core, other), y_at(1 - core, other), fws.at[k, d], fwr.at[k, other],
                    device_id=(row, col), device_id_type=MESH).wait_recv()
            for c in c3 + fw:
                c.wait_send()

    def last(chunk):
        at = pl.ds(pl.multiple_of(chunk * 256, 256), 256)
        return acc[at, :] + jnp.dot(k_mat[0, at, :], x_buf[0], preferred_element_type=F32)

    def to_partner(p):
        return pltpu.make_async_remote_copy(
            fs.at[p], fr.at[p], f1s.at[p], f1r.at[p], device_id=(row, partner), device_id_type=MESH)

    def to_owner(p):
        return pltpu.make_async_remote_copy(
            gs.at[p], gr.at[pos], f2s.at[p], f2r.at[pos], device_id=(row, p * 2 + core), device_id_type=MESH)

    def give(step):
        p = pos_at(step)
        fs[p] = last(p * 2 + 1 - core).astype(BF16)
        to_partner(p).start()

    order = FAR + ((0, 0),)
    give(order[0])
    give(order[1])
    for n, step in enumerate(FAR):
        p = pos_at(step)
        v = last(p * 2 + core)
        if n + 2 < len(order):
            give(order[n + 2])
        to_partner(p).wait_recv()
        gs[p] = (v + fr[p].astype(F32)).astype(BF16)
        to_owner(p).start()

    v = last(pos * 2 + core)
    to_partner(pos).wait_recv()
    v = v + fr[pos].astype(F32)
    for d in range(1, 8):
        other = (pos + d) % 8
        pltpu.make_async_remote_copy(
            gs.at[other], gr.at[other], f2s.at[other], f2r.at[other],
            device_id=(row, col), device_id_type=MESH).wait_recv()
        v = v + gr[other].astype(F32)
    pred[...] = v

    @pl.loop(1, 8)
    def _(d):
        p = (pos + d) % 8
        to_partner(p).wait_send()
        to_owner(p).wait_send()

    to_partner(pos).wait_send()


def finish(solved, scored, alpha, pred):
    alpha[...] = solved[...]
    pred[...] = scored[...]


def shards(factor_blocks, inverse_blocks, right_side, centers, owner_map, test_pool, test_rows):
    any_ = pl.BlockSpec(memory_space=pl.ANY)
    smem = pl.BlockSpec(memory_space=pltpu.SMEM)
    vmem = pl.BlockSpec(memory_space=pltpu.VMEM)
    V = pltpu.VMEM
    dma = pltpu.SemaphoreType.DMA
    scratch = [
        V((6, 4, 256, 2, 256), BF16), V((4, 2, 256, 4, 256), BF16), V((1024, 512), BF16), V((512, 1024), BF16),
        V((2, 512, 128), F32), V((4, 4, 256, 128), BF16), V((3, 4, 256, 128), BF16), V((8, 256, 512), BF16),
        V((8, 8, 256), F32), V((2, 1024, 512), BF16), V((6144 * 4, 128), F32), V((ROWS_ITEM * 4, 128), F32),
        V((2, ROWS_ITEM, 512), BF16), V((2, ROWS_ITEM, 128), F32),
        V((4, 4096, 512), BF16), V((4, 512, 128), BF16), V((512, 128), F32), V((4, 512, 128), BF16),
        V((4, 4, 128, 128), BF16), V((4, 8, 128, 128), BF16), V((1024, 128), F32), V((8, 128), F32),
        V((4, 512, 128), BF16), V((4, 512, 128), BF16), V((4, 512, 128), BF16), V((4, 8, 64, 128), BF16),
        V((4096, 128), F32), V((8, 256, 128), BF16), V((8, 256, 128), BF16), V((8, 256, 128), BF16),
        V((8, 256, 128), BF16),
        dma((8,)), dma((2,)), dma((4, 4)), dma((4, 4)), dma((4, 8)), dma((4, 8)), dma((4,)), dma((4,)),
        dma((4, 8)), dma((4, 8)), dma((4, 8)), dma((4, 8)), dma((4, 8)), dma((4, 8)),
        dma((8,)), dma((8,)), dma((8,)), dma((8,)),
    ]
    solved, scored = pl.pallas_call(
        kernel,
        out_shape=(
            jax.ShapeDtypeStruct((4, 2, 256, 128), F32),
            jax.ShapeDtypeStruct((256, 128), F32),
        ),
        in_specs=[smem, smem, any_, any_, any_, any_, any_],
        out_specs=(vmem, vmem),
        scratch_shapes=scratch,
        name="solve_and_score",
        compiler_params=pltpu.CompilerParams(
            collective_id=0, has_side_effects=True, vmem_limit_bytes=67043328
        ),
    )(owner_map.reshape(8), test_rows, factor_blocks, inverse_blocks, right_side, centers, test_pool)
    return pl.pallas_call(
        finish,
        out_shape=(
            jax.ShapeDtypeStruct((4, 2, 256, 128), F32),
            jax.ShapeDtypeStruct((256, 128), F32),
        ),
        in_specs=[vmem, vmem],
        out_specs=(vmem, vmem),
        name="finish",
    )(solved, scored)


def solution(mesh):
    in_specs = (
        P(None, None, "row", None, "col"),
        P(None, None, "col", None, "row"),
        P(None, None, "row", None),
        P(None, "col", None),
        P(None, "col"),
        P("row", None),
        P("row"),
    )
    out_specs = (P(None, None, "col", None), P(("row", "col"), None))
    return jax.shard_map(shards, mesh=mesh, in_specs=in_specs, out_specs=out_specs, check_vma=False)
```
